512 devices in a mesh: band: 16 (over x, y), region: 32 (over z, core).
Axes of the slice: x: 4, y: 4, z: 16, core: 2. Of those that a mesh axis runs over, the one named last changes fastest.
Arguments:
- state: bfloat16 [16, 32768], P(None, 'region'), may hold values from -4 to 4
- absorb_weight: bfloat16 [16, 16384], P(None, 'band'), may hold values from -1.5 to 1.5
- emit_weight: bfloat16 [16, 16384], P(None, 'band'), may hold values from -1.5 to 1.5
- path_len: float32 [8, 8192], P(None, 'region'), may hold values from 0.02 to 0.2
- crossing_slot: int32 [8, 8192], P(None, 'region'), may hold values from 0 to 4095, as said below
- request_rows: int32 [32, 32, 128], P('region'), may hold values from 0 to 1023
- cot_intensity: float32 [16384, 8192], P('band', 'region'), may hold values from -6 to 6
Outputs:
- grad_state: float32 [16, 32768], P(None, 'region')
The draws below stay inside these ranges and needn't reach their ends.
Inputs may be any that keep to these rules, and one draw needn't show every extreme that they name: `crossing_slot`: within each ray block (the 256 rays of one index of region) the 2048 crossings take distinct slots; slot p * 128 + s names the cell listed at request_rows[block, p, s]. In every draw one region has all 128 of its slots taken by every ray block; the other listed slots are partly unused.
All inputs are finite; a program needn't handle non-finite values.
Results may differ from the reference program's by a relative error of at most 0.0051.
Values may be sent and summed in bfloat16 or wider, within the bound.
No kernel may reach another device: no remote copies, remote signals or barrier semaphores. Data moves between devices by JAX's collectives and lax.ppermute only.
A program may use at most 64 MiB of HBM per device.

```python
import math
import jax
import jax.numpy as jnp
from jax import lax

NS = 16
BIN_DEV = 1024
LEN = 8
RAY_DEV = 256
CELL_DEV = 1024
SPEC = 16384
RAYS = 8192
CELLS = 32768
CAP = 128
N_BAND = 16
N_REGION = 32


def draw_crossing_slot(key, part):
    crossings = RAY_DEV * LEN
    pair_count = N_REGION * CAP
    hot_owner = jax.random.randint(jax.random.fold_in(key, 7), (), 0, N_REGION)
    slot_index = jnp.arange(pair_count, dtype=jnp.int32)
    owner_ids = slot_index // CAP
    at_ends = (slot_index == 0) | (slot_index == pair_count - 1)

    def one_block(requester):
        sub_key = jax.random.fold_in(key, 1000 + requester)
        ranking = jax.random.permutation(jax.random.fold_in(sub_key, 1), pair_count).astype(jnp.int32)
        priority = jnp.where(owner_ids == hot_owner, ranking - pair_count, ranking)
        priority = jnp.where(at_ends, slot_index - 3 * pair_count, priority)
        chosen = jnp.argsort(priority)[:crossings].astype(jnp.int32)
        shuffle = jax.random.permutation(jax.random.fold_in(sub_key, 2), crossings)
        return chosen[shuffle].reshape(LEN, RAY_DEV)
    blocks = jax.vmap(one_block)(jnp.arange(N_REGION, dtype=jnp.int32))
    return jnp.transpose(blocks, (1, 0, 2)).reshape(LEN, N_REGION * RAY_DEV).astype(jnp.int32)


def touch_ends(entries, stream_key, low, top_value):
    longest = entries.shape.index(max(entries.shape))
    spots = []
    for shift in (0, 1):
        where = [jax.random.randint(jax.random.fold_in(stream_key, axis), (), 0, length) for axis, length in enumerate(entries.shape)]
        where[longest] = (where[longest] + shift) % entries.shape[longest]
        spots.append(tuple(where))
    return entries.at[spots[0]].set(low).at[spots[1]].set(top_value)


def steps_of(rng, extent, shards, smallest, largest):
    level, own = 1.0, jax.random.fold_in(rng, 6)
    for dim, shards_of in shards:
        steps = jnp.exp(jax.random.uniform(jax.random.fold_in(own, dim), (shards_of,), jnp.float32, smallest / len(shards), largest / len(shards)))
        level = level * jnp.repeat(steps, extent[dim] // shards_of).reshape([-1 if axis == dim else 1 for axis in range(len(extent))])
    return level


def gaussian(rng, extent, scale, most, cuts=(), kind=jnp.bfloat16):
    factor_of = steps_of(rng, extent, cuts, -0.22, 0.18) if cuts else 1.0
    drawn = jax.random.normal(rng, extent, jnp.float32) * scale * factor_of
    return jnp.minimum(jnp.maximum(drawn, -most), most).astype(kind)


def setup_inputs(seed: int = 0) -> dict:
    seeds = jax.random.split(jax.random.key(seed), 8)
    return {
        "state": gaussian(seeds[0], (NS, CELLS), 1.0, 4.0, ((1, 32),)),
        "absorb_weight": gaussian(seeds[1], (NS, SPEC), NS ** -0.5, 1.5, ((1, 16),)),
        "emit_weight": gaussian(seeds[2], (NS, SPEC), NS ** -0.5, 1.5, ((1, 16),)),
        "path_len": jnp.clip(jnp.exp(math.log(0.2) - 2.3025851 * jax.random.uniform(seeds[3], (LEN, RAYS), jnp.float32) ** steps_of(seeds[3], (LEN, RAYS), ((1, 32),), -0.2, 0.2)), 0.02, 0.2),
        "crossing_slot": draw_crossing_slot(jax.random.fold_in(seeds[7], 71), 0),
        "request_rows": touch_ends(jax.random.randint(seeds[5], (N_REGION, N_REGION, CAP), 0, CELL_DEV), jax.random.fold_in(seeds[5], 1), 0, CELL_DEV - 1).astype(jnp.int32),
        "cot_intensity": gaussian(seeds[6], (SPEC, RAYS), 1.0, 6.0, ((0, 16), (1, 32)), jnp.float32),
    }


def adjoint_block(absorb_x, emit_x, length, cot_block, w_abs, w_emit):
    depth_step = absorb_x.astype(jnp.float32) * length[None]
    passed = jnp.cumsum(depth_step, axis=1) - depth_step
    transmit = jnp.exp(-passed)
    emitted = emit_x.astype(jnp.float32) * length[None] * transmit
    behind = lax.cumsum(emitted, axis=1, reverse=True) - emitted
    grad_emit = (cot_block[:, None, :] * emitted).astype(jnp.bfloat16)
    grad_absorb = (-cot_block[:, None, :] * depth_step * behind).astype(jnp.bfloat16)
    bin_count = grad_emit.shape[0]
    grad_emit = grad_emit.reshape(bin_count, -1)
    grad_absorb = grad_absorb.reshape(bin_count, -1)
    return jnp.dot(w_abs, grad_absorb, preferred_element_type=jnp.float32) + jnp.dot(w_emit, grad_emit, preferred_element_type=jnp.float32)


def reference(state, absorb_weight, emit_weight, path_len, crossing_slot, request_rows, cot_intensity):
    crossings = RAY_DEV * LEN

    def per_block(grad_cells, block_index):
        first_ray = (block_index * RAY_DEV).astype(jnp.int32)
        slot_ids = lax.dynamic_slice_in_dim(crossing_slot, first_ray, RAY_DEV, 1).reshape(-1)
        owner_ids = slot_ids // CAP
        within = slot_ids % CAP
        rows_block = lax.dynamic_index_in_dim(request_rows, block_index, 0, keepdims=False)
        local_rows = rows_block[owner_ids, within]
        cell_ids = (owner_ids * CELL_DEV + local_rows).astype(jnp.int32)
        state_x = jnp.take(state, cell_ids, axis=1)
        length = lax.dynamic_slice_in_dim(path_len, first_ray, RAY_DEV, 1)

        def per_band(grad_cross, band_index):
            first_bin = (band_index * BIN_DEV).astype(jnp.int32)
            w_abs = lax.dynamic_slice_in_dim(absorb_weight, first_bin, BIN_DEV, 1)
            w_emit = lax.dynamic_slice_in_dim(emit_weight, first_bin, BIN_DEV, 1)
            absorb_x = jnp.exp(jnp.dot(w_abs.T, state_x, preferred_element_type=jnp.float32)).astype(jnp.bfloat16)
            emit_x = jnp.exp(jnp.dot(w_emit.T, state_x, preferred_element_type=jnp.float32)).astype(jnp.bfloat16)
            cot_block = lax.dynamic_slice(cot_intensity, (first_bin, first_ray), (BIN_DEV, RAY_DEV))
            term = adjoint_block(absorb_x.reshape(BIN_DEV, LEN, RAY_DEV), emit_x.reshape(BIN_DEV, LEN, RAY_DEV), length, cot_block, w_abs, w_emit)
            return grad_cross + term, None

        grad_cross, _ = lax.scan(per_band, jnp.zeros((NS, crossings), jnp.float32), jnp.arange(N_BAND, dtype=jnp.int32))
        grad_cells = grad_cells.at[:, cell_ids].add(grad_cross)
        return grad_cells, None

    grad_state, _ = lax.scan(per_block, jnp.zeros((NS, CELLS), jnp.float32), jnp.arange(N_REGION, dtype=jnp.int32))
    return grad_state
```

```python
import math

import jax
import jax.numpy as jnp
import ml_dtypes
from jax import lax
from jax.experimental import pallas as pl
from jax.experimental.pallas import tpu as pltpu
from jax.sharding import PartitionSpec as P

NS = 16
BINS = 1024
LEN = 8
RAYS = 256
CROSS = LEN * RAYS
OWNERS = 32
CAP = 128
BANDS = 16
KX = 128
BLOCK = 256
SUB = 16
LOG2E = 1.0 / math.log(2.0)
LN2 = math.log(2.0)
VMEM_LIMIT = 48 << 20

f32 = jnp.float32
bf16 = jnp.bfloat16


def three_parts(x):
    high = x.astype(bf16).astype(f32)
    mid = (x - high).astype(bf16).astype(f32)
    low = (x - high - mid).astype(bf16).astype(f32)
    return high, mid, low


def prepare_kernel(
    slot_ref, rows_ref, len_ref, wa_ref, we_ref, slot_hot_ref, low_hot_ref, high_ref, tag_ref, ext_ref, w_ref
):
    rows = rows_ref[...]
    row_low = (rows & 127).astype(f32)
    row_high = (rows >> 7).astype(f32)
    listed = jnp.concatenate([row_low, row_high], axis=0).astype(bf16)
    for owner in range(OWNERS):
        line = lax.broadcasted_iota(jnp.int32, (8, CAP), 0)
        tag_ref[owner] = jnp.where(
            line == 0, row_low[owner : owner + 1], jnp.where(line == 1, row_high[owner : owner + 1], 0.0)
        ).astype(bf16)
    lines = lax.broadcasted_iota(jnp.int32, (128, RAYS), 0)
    owner_lines = lax.broadcasted_iota(jnp.int32, (OWNERS, RAYS), 0)
    ext_lines = lax.broadcasted_iota(jnp.int32, (16, RAYS), 0)
    for j in range(LEN):
        cols = slice(j * RAYS, (j + 1) * RAYS)
        slot = slot_ref[j : j + 1, :]
        owner = slot >> 7
        slot_hot = jnp.where(lines == (slot & 127), 1.0, 0.0).astype(bf16)
        slot_hot_ref[:, cols] = slot_hot
        found = jnp.dot(listed, slot_hot, preferred_element_type=f32)
        mine = owner_lines == owner
        low = jnp.sum(jnp.where(mine, found[:OWNERS], 0.0), axis=0, keepdims=True)
        high = jnp.sum(jnp.where(mine, found[OWNERS:], 0.0), axis=0, keepdims=True)
        low_hot_ref[:, cols] = jnp.where(lines == low.astype(jnp.int32), 1.0, 0.0).astype(bf16)
        high_ref[j : j + 1, :] = owner * 8 + high.astype(jnp.int32)
        l0, l1, l2 = three_parts(jnp.log(len_ref[j : j + 1, :]) * LOG2E)
        ext_ref[:, cols] = jnp.where(
            ext_lines == 0,
            l0,
            jnp.where(ext_lines == 1, l1, jnp.where(ext_lines == 2, l2, jnp.where(ext_lines < 6, 1.0, 0.0))),
        ).astype(bf16)
    consts = []
    rest = math.log2(LOG2E)
    for _ in range(3):
        part = float(ml_dtypes.bfloat16(rest))
        consts.append(part)
        rest -= part
    step = 128
    tail = lax.broadcasted_iota(jnp.int32, (KX - 2 * NS, step), 0)
    for which, ref in ((0, wa_ref), (1, we_ref)):
        c0, c1, c2 = consts if which == 0 else (0.0, 0.0, 0.0)
        extra = jnp.where(
            tail < 3,
            1.0,
            jnp.where(tail == 3, c0, jnp.where(tail == 4, c1, jnp.where(tail == 5, c2, 0.0))),
        )
        for first in range(0, BINS, step):
            scaled = ref[:, first : first + step].astype(f32) * LOG2E
            high = scaled.astype(bf16).astype(f32)
            stacked = jnp.concatenate([high, scaled - high, extra], axis=0)
            w_ref[which, first : first + step, :] = stacked.T.astype(bf16)


def gather_kernel(table_ref, low_hot_ref, high_ref, out_ref, row_ref):
    table = table_ref[...].reshape(OWNERS * 8, 128)
    lines = lax.broadcasted_iota(jnp.int32, (OWNERS * 8, RAYS), 0)
    for j in range(LEN):
        found = jnp.dot(table, low_hot_ref[:, j * RAYS : (j + 1) * RAYS], preferred_element_type=f32)
        mine = lines == high_ref[j : j + 1, :]
        value = jnp.sum(jnp.where(mine, found, 0.0), axis=0, keepdims=True)
        row_ref[2 * j : 2 * j + 1, :] = value[:, :128]
        row_ref[2 * j + 1 : 2 * j + 2, :] = value[:, 128:]
    value = row_ref[...].astype(bf16)
    for peer in range(BANDS):
        out_ref[peer] = value


def adjoint_kernel(
    states_ref,
    ext_ref,
    w_ref,
    wa_ref,
    we_ref,
    slot_ref,
    slot_hot_ref,
    tag_ref,
    cot_ref,
    out_ref,
    x_ref,
    la_ref,
    le_ref,
    ga_ref,
    ge_ref,
    sum_a_ref,
    sum_e_ref,
    spread_ref,
):
    step = pl.program_id(0)

    @pl.when(step == 0)
    def _():
        for tile in range(CROSS // 128):
            cols = slice(tile * 128, (tile + 1) * 128)
            x = states_ref[:, tile, :]
            x_ref[0:NS, cols] = x
            x_ref[NS : 2 * NS, cols] = x
        x_ref[2 * NS : 3 * NS, :] = ext_ref[...]
        x_ref[3 * NS :, :] = jnp.zeros((KX - 3 * NS, CROSS), bf16)
        sum_a_ref[...] = jnp.zeros_like(sum_a_ref)
        sum_e_ref[...] = jnp.zeros_like(sum_e_ref)

    la_ref[...] = jnp.dot(w_ref[0], x_ref[...], preferred_element_type=f32)
    le_ref[...] = jnp.dot(w_ref[1], x_ref[...], preferred_element_type=f32)
    for first in range(0, BLOCK, SUB):
        bins = slice(first, first + SUB)
        for half in range(2):
            cot = cot_ref[bins, half * 128 : (half + 1) * 128]
            depths, emitteds = [], []
            passed = jnp.zeros((SUB, 128), f32)
            for j in range(LEN):
                cols = slice(j * RAYS + half * 128, j * RAYS + half * 128 + 128)
                depth = jnp.exp2(la_ref[bins, cols])
                emitteds.append(cot * jnp.exp2(le_ref[bins, cols] - passed))
                depths.append(depth)
                passed = passed + depth
            behind = jnp.zeros((SUB, 128), f32)
            for j in reversed(range(LEN)):
                cols = slice(j * RAYS + half * 128, j * RAYS + half * 128 + 128)
                ge_ref[bins, cols] = emitteds[j].astype(bf16)
                ga_ref[bins, cols] = (depths[j] * behind).astype(bf16)
                behind = behind + emitteds[j]
    sum_a_ref[...] += jnp.dot(wa_ref[...], ga_ref[...], preferred_element_type=f32)
    sum_e_ref[...] += jnp.dot(we_ref[...], ge_ref[...], preferred_element_type=f32)

    @pl.when(step == pl.num_programs(0) - 1)
    def _():
        for j in range(LEN):
            cols = slice(j * RAYS, (j + 1) * RAYS)
            value = sum_e_ref[:, cols] - LN2 * sum_a_ref[:, cols]
            owner = slot_ref[j : j + 1, :] >> 7
            for p in range(OWNERS):
                spread_ref[p * NS : (p + 1) * NS, cols] = jnp.where(owner == p, value, 0.0).astype(bf16)
        placed = lax.dot_general(
            spread_ref[...], slot_hot_ref[...], (((1,), (1,)), ((), ())), preferred_element_type=f32
        )
        for p in range(OWNERS):
            out_ref[p, 0:NS, :] = placed[p * NS : (p + 1) * NS].astype(bf16)
            out_ref[p, NS : NS + 8, :] = tag_ref[p]


def scatter_kernel(got_ref, out_ref, value_ref, low_hot_ref):
    lines = lax.broadcasted_iota(jnp.int32, (128, CAP), 0)
    for q in range(OWNERS):
        cols = slice(q * CAP, (q + 1) * CAP)
        value = got_ref[q, 0:NS, :].astype(f32)
        tags = got_ref[q, NS : NS + 8, :].astype(f32)
        low = tags[0:1, :].astype(jnp.int32)
        high = tags[1:2, :].astype(jnp.int32)
        low_hot_ref[:, cols] = jnp.where(lines == low, 1.0, 0.0).astype(bf16)
        for h in range(8):
            value_ref[h * NS : (h + 1) * NS, cols] = jnp.where(high == h, value, 0.0).astype(bf16)
    total = lax.dot_general(
        value_ref[...], low_hot_ref[...], (((1,), (1,)), ((), ())), preferred_element_type=f32
    )
    for h in range(8):
        part = total[h * NS : (h + 1) * NS].astype(bf16)
        for peer in range(BANDS):
            out_ref[peer, :, h * 128 : (h + 1) * 128] = part


def sum_kernel(part_ref, out_ref):
    total = part_ref[0].astype(f32)
    for peer in range(1, BANDS):
        total = total + part_ref[peer].astype(f32)
    out_ref[...] = total


def shape(dims, dtype):
    return jax.ShapeDtypeStruct(dims, dtype)


PARAMS = pltpu.CompilerParams(vmem_limit_bytes=VMEM_LIMIT)


def on_device(
    state, absorb_weight, emit_weight, path_len, crossing_slot, request_rows, cot_intensity
):
    band = lax.axis_index("band")
    mine = lax.dynamic_slice_in_dim(state, band, 1, axis=0).reshape(1, 8, 128)
    table = lax.all_to_all(
        jnp.broadcast_to(mine, (OWNERS, 8, 128)), "region", split_axis=0, concat_axis=0, tiled=True
    )
    slot_hot, low_hot, high, tags, ext, weights = pl.pallas_call(
        prepare_kernel,
        out_shape=(
            shape((128, CROSS), bf16),
            shape((128, CROSS), bf16),
            shape((LEN, RAYS), jnp.int32),
            shape((OWNERS, 8, CAP), bf16),
            shape((NS, CROSS), bf16),
            shape((2, BINS, KX), bf16),
        ),
        compiler_params=PARAMS,
        cost_estimate=pl.CostEstimate(flops=40_000_000, bytes_accessed=2_000_000, transcendentals=4096),
    )(crossing_slot, request_rows.reshape(OWNERS, CAP), path_len, absorb_weight, emit_weight)
    picked = pl.pallas_call(
        gather_kernel,
        out_shape=shape((BANDS, NS, 128), bf16),
        scratch_shapes=[pltpu.VMEM((CROSS // 128, 128), f32)],
        compiler_params=PARAMS,
    )(table, low_hot, high)
    states = lax.all_to_all(picked, "band", split_axis=0, concat_axis=0, tiled=True)
    whole = lambda *dims: pl.BlockSpec(dims, lambda i: (0,) * len(dims))
    sending = pl.pallas_call(
        adjoint_kernel,
        grid=(BINS // BLOCK,),
        in_specs=[
            whole(NS, CROSS // 128, 128),
            whole(NS, CROSS),
            pl.BlockSpec((2, BLOCK, KX), lambda i: (0, i, 0)),
            pl.BlockSpec((NS, BLOCK), lambda i: (0, i)),
            pl.BlockSpec((NS, BLOCK), lambda i: (0, i)),
            whole(LEN, RAYS),
            whole(128, CROSS),
            whole(OWNERS, 8, CAP),
            pl.BlockSpec((BLOCK, RAYS), lambda i: (i, 0)),
        ],
        out_specs=whole(OWNERS, NS + 8, CAP),
        out_shape=shape((OWNERS, NS + 8, CAP), bf16),
        scratch_shapes=[
            pltpu.VMEM((KX, CROSS), bf16),
            pltpu.VMEM((BLOCK, CROSS), f32),
            pltpu.VMEM((BLOCK, CROSS), f32),
            pltpu.VMEM((BLOCK, CROSS), bf16),
            pltpu.VMEM((BLOCK, CROSS), bf16),
            pltpu.VMEM((NS, CROSS), f32),
            pltpu.VMEM((NS, CROSS), f32),
            pltpu.VMEM((OWNERS * NS, CROSS), bf16),
        ],
        compiler_params=PARAMS,
    )(
        states,
        ext,
        weights,
        absorb_weight,
        emit_weight,
        crossing_slot,
        slot_hot,
        tags,
        cot_intensity,
    )
    returned = lax.all_to_all(sending, "region", split_axis=0, concat_axis=0, tiled=True)
    partial = pl.pallas_call(
        scatter_kernel,
        out_shape=shape((BANDS, NS, 1024), bf16),
        scratch_shapes=[pltpu.VMEM((128, OWNERS * CAP), bf16), pltpu.VMEM((128, OWNERS * CAP), bf16)],
        compiler_params=PARAMS,
    )(returned)
    parts = lax.all_to_all(partial, "band", split_axis=0, concat_axis=0, tiled=True)
    return pl.pallas_call(
        sum_kernel, out_shape=shape((NS, 1024), f32), compiler_params=PARAMS
    )(parts)


def solution(mesh):
    return jax.shard_map(
        on_device,
        mesh=mesh,
        in_specs=(
            P(None, "region"),
            P(None, "band"),
            P(None, "band"),
            P(None, "region"),
            P(None, "region"),
            P("region", None, None),
            P("band", "region"),
        ),
        out_specs=P(None, "region"),
        check_vma=False,
    )
```

```python
import math

import jax
import jax.numpy as jnp
import ml_dtypes
from jax import lax
from jax.experimental import pallas as pl
from jax.experimental.pallas import tpu as pltpu
from jax.sharding import PartitionSpec as P

NS = 16
BINS = 1024
LEN = 8
RAYS = 256
CROSS = LEN * RAYS
OWNERS = 32
CAP = 128
BANDS = 16
KX = 48
KW = 128
BLOCK = 128
SUB = 16
LOG2E = 1.0 / math.log(2.0)
LN2 = math.log(2.0)
VMEM_LIMIT = 48 << 20

f32 = jnp.float32
bf16 = jnp.bfloat16


def three_parts(x):
    high = x.astype(bf16).astype(f32)
    mid = (x - high).astype(bf16).astype(f32)
    low = (x - high - mid).astype(bf16).astype(f32)
    return high, mid, low


def component_kernel(state_ref, out_ref):
    band = lax.axis_index("band")
    mine = lax.broadcasted_iota(jnp.int32, (NS, 128), 0) == band
    rows = []
    for h in range(8):
        part = state_ref[:, h * 128 : (h + 1) * 128].astype(f32)
        rows.append(jnp.sum(jnp.where(mine, part, 0.0), axis=0, keepdims=True))
    value = jnp.concatenate(rows, axis=0).astype(bf16)
    for region in range(OWNERS):
        out_ref[region] = value


def prepare_kernel(
    slot_ref, rows_ref, len_ref, wa_ref, we_ref, slot_hot_ref, low_hot_ref, high_ref, tag_ref, ext_ref, w_ref
):
    rows = rows_ref[...]
    row_low = (rows & 127).astype(f32)
    row_high = (rows >> 7).astype(f32)
    listed = jnp.concatenate([row_low, row_high], axis=0).astype(bf16)
    for owner in range(OWNERS):
        tag_ref[owner] = jnp.concatenate(
            [row_low[owner : owner + 1], row_high[owner : owner + 1]], axis=0
        ).astype(bf16)
    lines = lax.broadcasted_iota(jnp.int32, (128, RAYS), 0)
    wide_lines = lax.broadcasted_iota(jnp.int32, (2 * CAP, RAYS), 0)
    owner_lines = lax.broadcasted_iota(jnp.int32, (OWNERS, RAYS), 0)
    ext_lines = lax.broadcasted_iota(jnp.int32, (16, RAYS), 0)
    for j in range(LEN):
        cols = slice(j * RAYS, (j + 1) * RAYS)
        slot = slot_ref[j : j + 1, :]
        owner = slot >> 7
        slot_hot = jnp.where(lines == (slot & 127), 1.0, 0.0).astype(bf16)
        slot_hot_ref[:, cols] = jnp.where(wide_lines == (slot & 255), 1.0, 0.0).astype(bf16)
        found = jnp.dot(listed, slot_hot, preferred_element_type=f32)
        mine = owner_lines == owner
        low = jnp.sum(jnp.where(mine, found[:OWNERS], 0.0), axis=0, keepdims=True)
        high = jnp.sum(jnp.where(mine, found[OWNERS:], 0.0), axis=0, keepdims=True)
        low_hot_ref[:, cols] = jnp.where(lines == low.astype(jnp.int32), 1.0, 0.0).astype(bf16)
        high_ref[j : j + 1, :] = owner * 8 + high.astype(jnp.int32)
        l0, l1, l2 = three_parts(jnp.log(len_ref[j : j + 1, :]) * LOG2E)
        ext_ref[:, cols] = jnp.where(
            ext_lines == 0,
            l0,
            jnp.where(ext_lines == 1, l1, jnp.where(ext_lines == 2, l2, jnp.where(ext_lines < 6, 1.0, 0.0))),
        ).astype(bf16)
    consts = []
    rest = math.log2(LOG2E)
    for _ in range(3):
        part = float(ml_dtypes.bfloat16(rest))
        consts.append(part)
        rest -= part
    step = 128
    tail = lax.broadcasted_iota(jnp.int32, (KW - 2 * NS, step), 0)
    for which, ref in ((0, wa_ref), (1, we_ref)):
        c0, c1, c2 = consts if which == 0 else (0.0, 0.0, 0.0)
        extra = jnp.where(
            tail < 3,
            1.0,
            jnp.where(tail == 3, c0, jnp.where(tail == 4, c1, jnp.where(tail == 5, c2, 0.0))),
        )
        for first in range(0, BINS, step):
            scaled = ref[:, first : first + step].astype(f32) * LOG2E
            high = scaled.astype(bf16).astype(f32)
            stacked = jnp.concatenate([high, scaled - high, extra], axis=0)
            w_ref[which, first : first + step, :] = stacked.T.astype(bf16)


def gather_kernel(table_ref, low_hot_ref, high_ref, out_ref, row_ref):
    table = table_ref[...].reshape(OWNERS * 8, 128)
    lines = lax.broadcasted_iota(jnp.int32, (OWNERS * 8, RAYS), 0)
    for j in range(LEN):
        found = jnp.dot(table, low_hot_ref[:, j * RAYS : (j + 1) * RAYS], preferred_element_type=f32)
        mine = lines == high_ref[j : j + 1, :]
        value = jnp.sum(jnp.where(mine, found, 0.0), axis=0, keepdims=True)
        row_ref[2 * j : 2 * j + 1, :] = value[:, :128]
        row_ref[2 * j + 1 : 2 * j + 2, :] = value[:, 128:]
    value = row_ref[...].astype(bf16)
    for peer in range(BANDS):
        out_ref[peer] = value


def adjoint_kernel(
    states_ref,
    ext_ref,
    w_ref,
    wa_ref,
    we_ref,
    slot_ref,
    slot_hot_ref,
    tag_ref,
    cot_ref,
    out_ref,
    x_ref,
    la0_ref,
    la1_ref,
    le0_ref,
    le1_ref,
    ga0_ref,
    ga1_ref,
    ge0_ref,
    ge1_ref,
    sum_a_ref,
    sum_e_ref,
    spread_ref,
):
    la_refs, le_refs = (la0_ref, la1_ref), (le0_ref, le1_ref)
    ga_refs, ge_refs = (ga0_ref, ga1_ref), (ge0_ref, ge1_ref)
    blocks = BINS // BLOCK
    for tile in range(CROSS // 128):
        cols = slice(tile * 128, (tile + 1) * 128)
        x = states_ref[:, tile, :]
        x_ref[0:NS, cols] = x
        x_ref[NS : 2 * NS, cols] = x
    x_ref[2 * NS : 3 * NS, :] = ext_ref[...]

    def logits(block, j):
        bins = slice(block * BLOCK, (block + 1) * BLOCK)
        cols = slice(j * RAYS, (j + 1) * RAYS)
        x = x_ref[:, cols]
        if j < LEN - 1:
            la_refs[block % 2][:, cols] = jnp.dot(w_ref[0, bins, :KX], x, preferred_element_type=f32)
        le_refs[block % 2][:, cols] = jnp.dot(w_ref[1, bins, :KX], x, preferred_element_type=f32)

    def contract(block, j):
        bins = slice(block * BLOCK, (block + 1) * BLOCK)
        cols = slice(j * RAYS, (j + 1) * RAYS)
        for w, g_refs, sum_ref in ((wa_ref, ga_refs, sum_a_ref), (we_ref, ge_refs, sum_e_ref)):
            if w is wa_ref and j == LEN - 1:
                continue
            part = jnp.dot(w[:, bins], g_refs[block % 2][:, cols], preferred_element_type=f32)
            sum_ref[:, cols] = part if block == 0 else sum_ref[:, cols] + part

    def adjoint(block, first, half):
        la_ref, le_ref = la_refs[block % 2], le_refs[block % 2]
        ga_ref, ge_ref = ga_refs[block % 2], ge_refs[block % 2]
        bins = slice(first, first + SUB)
        cot = cot_ref[block * BLOCK + first : block * BLOCK + first + SUB, half * 128 : (half + 1) * 128]
        depths, emitteds = [], []
        passed = None
        for j in range(LEN):
            cols = slice(j * RAYS + half * 128, j * RAYS + half * 128 + 128)
            power = le_ref[bins, cols]
            emitteds.append(cot * jnp.exp2(power if passed is None else power - passed))
            if j < LEN - 1:
                depth = jnp.exp2(la_ref[bins, cols])
                depths.append(depth)
                passed = depth if passed is None else passed + depth
        behind = None
        for j in reversed(range(LEN)):
            cols = slice(j * RAYS + half * 128, j * RAYS + half * 128 + 128)
            ge_ref[bins, cols] = emitteds[j].astype(bf16)
            if behind is None:
                behind = emitteds[j]
            else:
                ga_ref[bins, cols] = (depths[j] * behind).astype(bf16)
                behind = behind + emitteds[j]

    for j in range(LEN):
        logits(0, j)
    for block in range(blocks):
        units = [(first, half) for first in range(0, BLOCK, SUB) for half in range(2)]
        matmuls = []
        for j in range(LEN):
            if block + 1 < blocks:
                matmuls.append((logits, block + 1, j))
            if block > 0:
                matmuls.append((contract, block - 1, j))
        done = 0
        for index, (first, half) in enumerate(units):
            while done * len(units) < len(matmuls) * (index + 1) and done < len(matmuls):
                f, which, j = matmuls[done]
                f(which, j)
                done += 1
            adjoint(block, first, half)
    for j in range(LEN):
        contract(blocks - 1, j)

    for j in range(LEN):
        cols = slice(j * RAYS, (j + 1) * RAYS)
        value = sum_e_ref[:, cols]
        if j < LEN - 1:
            value = value - LN2 * sum_a_ref[:, cols]
        pair = slot_ref[j : j + 1, :] >> 8
        for p in range(OWNERS // 2):
            spread_ref[p * NS : (p + 1) * NS, cols] = jnp.where(pair == p, value, 0.0).astype(bf16)
    placed = lax.dot_general(
        spread_ref[...], slot_hot_ref[...], (((1,), (1,)), ((), ())), preferred_element_type=f32
    ).astype(bf16)
    for p in range(OWNERS):
        rows = slice((p // 2) * NS, (p // 2 + 1) * NS)
        mine = placed[rows, (p % 2) * CAP : (p % 2 + 1) * CAP]
        out_ref[9 * p : 9 * p + 8] = mine.reshape(NS // 2, 2, CAP)
        out_ref[9 * p + 8] = tag_ref[p]


def scatter_kernel(got_ref, out_ref, value_ref, low_hot_ref):
    lines = lax.broadcasted_iota(jnp.int32, (128, CAP), 0)
    for q in range(OWNERS):
        cols = slice(q * CAP, (q + 1) * CAP)
        value = got_ref[9 * q : 9 * q + 8].reshape(NS, CAP).astype(f32)
        tags = got_ref[9 * q + 8].astype(f32)
        low = tags[0:1, :].astype(jnp.int32)
        high = tags[1:2, :].astype(jnp.int32)
        low_hot_ref[:, cols] = jnp.where(lines == low, 1.0, 0.0).astype(bf16)
        for h in range(8):
            value_ref[h * NS : (h + 1) * NS, cols] = jnp.where(high == h, value, 0.0).astype(bf16)
    total = lax.dot_general(
        value_ref[...], low_hot_ref[...], (((1,), (1,)), ((), ())), preferred_element_type=f32
    )
    for h in range(8):
        part = total[h * NS : (h + 1) * NS].astype(bf16)
        for peer in range(BANDS):
            out_ref[peer, :, h * 128 : (h + 1) * 128] = part


def sum_kernel(part_ref, out_ref):
    total = part_ref[0].astype(f32)
    for peer in range(1, BANDS):
        total = total + part_ref[peer].astype(f32)
    out_ref[...] = total


def shape(dims, dtype):
    return jax.ShapeDtypeStruct(dims, dtype)


PARAMS = pltpu.CompilerParams(vmem_limit_bytes=VMEM_LIMIT)


def call(kernel, out_shape, **kwargs):
    return pl.pallas_call(kernel, out_shape=out_shape, compiler_params=PARAMS, **kwargs)


def prepare(crossing_slot, rows, path_len, absorb_weight, emit_weight):
    return call(
        prepare_kernel,
        (
            shape((2 * CAP, CROSS), bf16),
            shape((128, CROSS), bf16),
            shape((LEN, RAYS), jnp.int32),
            shape((OWNERS, 2, CAP), bf16),
            shape((NS, CROSS), bf16),
            shape((2, BINS, KW), bf16),
        ),
        cost_estimate=pl.CostEstimate(flops=40_000_000, bytes_accessed=2_000_000, transcendentals=4096),
    )(crossing_slot, rows, path_len, absorb_weight, emit_weight)


def adjoint(states, prepared, absorb_weight, emit_weight, crossing_slot, cot_intensity):
    slot_hot, _, _, tags, ext, weights = prepared
    return call(
        adjoint_kernel,
        shape((OWNERS * 9, 2, CAP), bf16),
        scratch_shapes=[pltpu.VMEM((KX, CROSS), bf16)]
        + [pltpu.VMEM((BLOCK, CROSS), f32)] * 4
        + [pltpu.VMEM((BLOCK, CROSS), bf16)] * 4
        + [pltpu.VMEM((NS, CROSS), f32)] * 2
        + [pltpu.VMEM((OWNERS // 2 * NS, CROSS), bf16)],
    )(
        states,
        ext,
        weights,
        absorb_weight,
        emit_weight,
        crossing_slot,
        slot_hot,
        tags,
        cot_intensity,
    )


def on_device(
    state, absorb_weight, emit_weight, path_len, crossing_slot, request_rows, cot_intensity
):
    component = call(component_kernel, shape((OWNERS, 8, 128), bf16))(state)
    table = lax.all_to_all(component, "region", split_axis=0, concat_axis=0, tiled=True)
    prepared = prepare(
        crossing_slot, request_rows.reshape(OWNERS, CAP), path_len, absorb_weight, emit_weight
    )
    picked = call(
        gather_kernel,
        shape((BANDS, NS, 128), bf16),
        scratch_shapes=[pltpu.VMEM((CROSS // 128, 128), f32)],
    )(table, prepared[1], prepared[2])
    states = lax.all_to_all(picked, "band", split_axis=0, concat_axis=0, tiled=True)
    sending = adjoint(states, prepared, absorb_weight, emit_weight, crossing_slot, cot_intensity)
    returned = lax.all_to_all(sending, "region", split_axis=0, concat_axis=0, tiled=True)
    partial = call(
        scatter_kernel,
        shape((BANDS, NS, 1024), bf16),
        scratch_shapes=[pltpu.VMEM((128, OWNERS * CAP), bf16), pltpu.VMEM((128, OWNERS * CAP), bf16)],
    )(returned)
    parts = lax.all_to_all(partial, "band", split_axis=0, concat_axis=0, tiled=True)
    return call(sum_kernel, shape((NS, 1024), f32))(parts)


def solution(mesh):
    return jax.shard_map(
        on_device,
        mesh=mesh,
        in_specs=(
            P(None, "region"),
            P(None, "band"),
            P(None, "band"),
            P(None, "region"),
            P(None, "region"),
            P("region", None, None),
            P("band", "region"),
        ),
        out_specs=P(None, "region"),
        check_vma=False,
    )
```
